32 devices in a mesh: dp: 4 (over x, core), expert: 8 (over z, y).
Axes of the slice: x: 2, y: 2, z: 4, core: 2. Of those that a mesh axis runs over, the one named last changes fastest.
Arguments:
- tokens: bfloat16 [4096, 2048], P(('dp', 'expert')), may hold values from -6 to 6
- cotangent: bfloat16 [4096, 2048], P(('dp', 'expert')), may hold values from -1.5 to 1.5
- gate_score: bfloat16 [4096], P(('dp', 'expert')), may hold values from 0.19921875 to 1
- block_expert: int32 [256], P(('dp', 'expert')), may hold values from 0 to 7, as said below
- expert_slot: int32 [8], replicated, may hold values from 0 to 7, each once
- up_weight: bfloat16 [8, 2048, 704], P('expert'), may hold values from -0.125 to 0.125
- down_weight: bfloat16 [8, 2048, 704], P('expert'), may hold values from -0.21875 to 0.21875
Outputs:
- token_grad: bfloat16 [4096, 2048], P(('dp', 'expert'))
- gate_grad: bfloat16 [4096], P(('dp', 'expert'))
- grad_up: bfloat16 [8, 2048, 704], P('expert', 'dp')
- grad_down: bfloat16 [8, 2048, 704], P('expert', 'dp')
The draws below stay inside these ranges and needn't reach their ends.
Inputs may be any that keep to these rules, and one draw needn't show every extreme that they name: `block_expert`: the 8 blocks of each device name every expert exactly once. `expert_slot`: each slot holds exactly one expert.
All inputs are finite; a program needn't handle non-finite values.
Results may differ from the reference program's by a relative error of at most 0.0085.
Values may be sent and summed in bfloat16 or wider, within the bound.
A program may use at most 64 MiB of HBM per device.

```python
import math
import jax
import jax.numpy as jnp
from jax import lax

D = 2048
H = 704
EXPERTS = 8
BLOCK = 16
TOKENS = 4096
BLOCKS = 256
N_DP = 4
N_EXPERT = 8


def draw_block_expert(key, part):
    group_keys = jax.random.split(key, BLOCKS // EXPERTS)
    orders = jax.vmap(lambda group_key: jax.random.permutation(group_key, EXPERTS))(group_keys)
    return orders.reshape(-1).astype(jnp.int32)


def level_of(own_key, shape, pieces, low, largest):
    level = 1.0
    for position, shards_of in pieces:
        heights = jax.random.uniform(jax.random.fold_in(jax.random.fold_in(own_key, 6), position), (shards_of,), jnp.float32, low / len(pieces), largest / len(pieces))
        level = level * jnp.repeat(jnp.exp(heights), shape[position] // shards_of).reshape((-1,) + (1,) * (len(shape) - 1 - position))
    return level


def gaussian(own_key, dims, scale, bound, shards=(), dtype=jnp.bfloat16):
    array = jax.random.normal(own_key, dims, jnp.float32) * scale
    if len(shards) > 0:
        array = level_of(own_key, dims, shards, -0.22, 0.18) * array
    return jnp.clip(array, min=-bound, max=bound).astype(dtype)


def setup_inputs(seed: int = 0) -> dict:
    streams_of = jax.random.split(jax.random.key(seed), 8)
    tokens = gaussian(streams_of[0], (TOKENS, D), 1.0, 6.0, ((0, 32),))
    cotangent = gaussian(streams_of[1], (TOKENS, D), 0.25, 1.5, ((0, 32),))
    gate_score = jnp.clip(jnp.exp(math.log(1.0) - 1.6133518 * jax.random.uniform(streams_of[2], (TOKENS,), jnp.float32) ** level_of(streams_of[2], (TOKENS,), ((0, 32),), -0.2, 0.2)), 0.19921875, 1.0).astype(jnp.bfloat16)
    block_expert = draw_block_expert(jax.random.fold_in(streams_of[7], 71), 0)
    expert_slot = jax.random.permutation(streams_of[4], EXPERTS).astype(jnp.int32)
    up_weight = gaussian(streams_of[5], (EXPERTS, D, H), D ** -0.5, 0.125, ((0, 8),))
    down_weight = gaussian(streams_of[6], (EXPERTS, D, H), H ** -0.5, 0.21875, ((0, 8),))
    return {"tokens": tokens, "cotangent": cotangent, "gate_score": gate_score, "block_expert": block_expert, "expert_slot": expert_slot, "up_weight": up_weight, "down_weight": down_weight}


def silu_slope(pre_act):
    logistic = jax.nn.sigmoid(pre_act)
    return logistic * (1.0 + pre_act * (1.0 - logistic))


def pick_blocks(values, order_index):
    return jax.vmap(jax.vmap(lambda table, picks: jnp.take(table, picks, axis=0)))(values, order_index)


def reference(tokens, cotangent, gate_score, block_expert, expert_slot, up_weight, down_weight):
    peer_count = N_EXPERT
    group_count = N_DP
    block_rows = BLOCK
    block_slot = jnp.take(expert_slot, block_expert).astype(jnp.int32).reshape(group_count, peer_count, peer_count)
    ordering = jnp.argsort(block_slot, axis=-1).astype(jnp.int32)

    def arrange(values):
        shaped = values.reshape((group_count, peer_count, peer_count, block_rows) + values.shape[1:])
        return jnp.moveaxis(pick_blocks(shaped, ordering), 2, 0)

    def restore(values):
        shaped = values.reshape((EXPERTS, group_count, peer_count, block_rows) + values.shape[2:])
        placed = pick_blocks(jnp.moveaxis(shaped, 0, 2), block_slot)
        return placed.reshape((TOKENS,) + values.shape[2:])

    contract_last = (((1,), (1,)), ((), ()))

    def expert(operands):
        slot_tokens, slot_cot, slot_gate, up_mat, down_mat = operands
        inputs = slot_tokens.reshape(-1, D)
        upstream = slot_cot.reshape(-1, D)
        gate_rows = slot_gate.reshape(-1)
        pre_act = jnp.dot(inputs, up_mat, preferred_element_type=jnp.float32)
        hidden = jax.nn.silu(pre_act).astype(jnp.bfloat16)
        expert_out = lax.dot_general(hidden, down_mat, contract_last, preferred_element_type=jnp.float32)
        gate_grad = jnp.sum(upstream.astype(jnp.float32) * expert_out, axis=1).astype(jnp.bfloat16)
        scaled = (gate_rows.astype(jnp.float32)[:, None] * upstream.astype(jnp.float32)).astype(jnp.bfloat16)
        hidden_grad = jnp.dot(scaled, down_mat, preferred_element_type=jnp.float32)
        pre_grad = (hidden_grad * silu_slope(pre_act)).astype(jnp.bfloat16)
        input_grad = lax.dot_general(pre_grad, up_mat, contract_last, preferred_element_type=jnp.float32).astype(jnp.bfloat16)
        input_groups = inputs.reshape(group_count, -1, D).astype(jnp.float32)
        scaled_groups = scaled.reshape(group_count, -1, D).astype(jnp.float32)
        pre_groups = pre_grad.reshape(group_count, -1, H).astype(jnp.float32)
        hidden_groups = hidden.reshape(group_count, -1, H).astype(jnp.float32)
        up_part = jnp.einsum("grd,grh->gdh", input_groups, pre_groups).astype(jnp.bfloat16)
        down_part = jnp.einsum("grd,grh->gdh", scaled_groups, hidden_groups).astype(jnp.bfloat16)
        grad_up = jnp.sum(up_part.astype(jnp.float32), axis=0).astype(jnp.bfloat16)
        grad_down = jnp.sum(down_part.astype(jnp.float32), axis=0).astype(jnp.bfloat16)
        return input_grad, gate_grad, grad_up, grad_down

    input_grad, gate_grad, grad_up, grad_down = lax.map(
        expert, (arrange(tokens), arrange(cotangent), arrange(gate_score), up_weight, down_weight))
    return restore(input_grad), restore(gate_grad), grad_up, grad_down
```

```python
import functools

import jax
import jax.numpy as jnp
from jax import lax
from jax.experimental import pallas as pl
from jax.experimental.pallas import tpu as pltpu
from jax.sharding import PartitionSpec as P

MESH = pl.DeviceIdType.MESH
RETURN_CHUNKS = 2


def fused_kernel(
    n_dp, n_ex,
    block_expert, expert_slot, gate_ref, tok_ref, cot_ref, up_hbm, down_hbm,
    tg_ref, gg_ref, gu_ref, gd_ref,
    up, down, gcol, stage_t, stage_s, recv_t, recv_s, cols_t, cols_s,
    hid, pgr, slope, stage_o, ret, gate_stage, gret,
    w_sem, t_send, t_recv, s_send, s_recv, ct_send, ct_recv, cs_send, cs_recv,
    h_send, h_recv, p_send, p_recv, r_send, r_recv, g_send, g_recv,
):
    blocks, rows, width = tok_ref.shape
    total = blocks * rows
    hidden_width = up.shape[1]
    share = width // n_dp
    g = lax.axis_index("dp")
    e = lax.axis_index("expert")
    up_copy = pltpu.make_async_copy(up_hbm.at[0], up, w_sem.at[0])
    down_copy = pltpu.make_async_copy(down_hbm.at[0], down, w_sem.at[1])
    up_copy.start()
    down_copy.start()

    steps = sorted(range(1, n_ex), key=lambda k: abs(2 * k - n_ex))
    peers = [lax.rem(e + k, n_ex) for k in steps]
    sources = [lax.rem(e + n_ex - k, n_ex) for k in steps]
    dp_steps = sorted(range(1, n_dp), key=lambda k: abs(2 * k - n_dp))
    dp_peers = [lax.rem(g + k, n_dp) for k in dp_steps]
    dp_sources = [lax.rem(g + n_dp - k, n_dp) for k in dp_steps]

    barrier = pltpu.get_barrier_semaphore()
    for peer in peers:
        pl.semaphore_signal(barrier, inc=1, device_id=(g, peer), device_id_type=MESH)
    for peer in dp_peers:
        pl.semaphore_signal(barrier, inc=1, device_id=(peer, e), device_id_type=MESH)

    slots = [expert_slot[block_expert[b]] for b in range(blocks)]

    def source_block(slot):
        found = jnp.int32(0)
        for b in range(blocks):
            found = jnp.where(slots[b] == slot, jnp.int32(b), found)
        return found

    own_block = source_block(e)
    picks = [source_block(peer) for peer in peers]

    gate_row = gate_ref[...].astype(jnp.float32)
    row_id = lax.broadcasted_iota(jnp.int32, (total, total), 0)
    lane_id = lax.broadcasted_iota(jnp.int32, (total, total), 1)
    column = jnp.sum(jnp.where(row_id == lane_id, gate_row, 0.0), axis=1, keepdims=True)
    gcol[...] = jnp.broadcast_to(column, (total, 128)).reshape(blocks, rows, 128)

    for i, pick in enumerate(picks):
        stage_t[i] = tok_ref[pick]
    pl.semaphore_wait(barrier, n_ex - 1 + n_dp - 1)

    sends = []

    def push(src, dst, send_sem, recv_sem, device):
        copy = pltpu.make_async_remote_copy(
            src_ref=src, dst_ref=dst, send_sem=send_sem, recv_sem=recv_sem,
            device_id=device, device_id_type=MESH)
        copy.start()
        sends.append(copy)

    def arrived(ref, send_sem, recv_sem):
        pltpu.make_async_remote_copy(
            src_ref=ref, dst_ref=ref, send_sem=send_sem, recv_sem=recv_sem,
            device_id=(g, peers[0]), device_id_type=MESH).wait_recv()

    for i, peer in enumerate(peers):
        push(stage_t.at[i], recv_t.at[e], t_send.at[i], t_recv.at[e], (g, peer))

    def scale(pick):
        factor = gcol[pick][:, :1]
        return (cot_ref[pick].astype(jnp.float32) * factor).astype(jnp.bfloat16)

    for i, peer in enumerate(peers):
        stage_s[i] = scale(picks[i])
        push(stage_s.at[i], recv_s.at[e], s_send.at[i], s_recv.at[e], (g, peer))
    recv_t[e] = tok_ref[own_block]
    recv_s[e] = scale(own_block)

    def forward(recv, cols, block, send_sem, recv_sem, i):
        for d, peer in enumerate(dp_peers):
            window = pl.ds(pl.multiple_of(peer * share, share), share)
            push(recv.at[block, :, window], cols.at[g, block],
                 send_sem.at[d, i], recv_sem.at[g, block], (peer, e))

    own = pl.ds(pl.multiple_of(g * share, share), share)

    forward(recv_t, cols_t, e, ct_send, ct_recv, n_ex - 1)
    forward(recv_s, cols_s, e, cs_send, cs_recv, n_ex - 1)
    for i, source in enumerate(sources):
        arrived(recv_t.at[source], t_send.at[i], t_recv.at[source])
        forward(recv_t, cols_t, source, ct_send, ct_recv, i)
    up_copy.wait()
    pre = jnp.dot(recv_t[...].reshape(total, width), up[...],
                  preferred_element_type=jnp.float32)
    logistic = 1.0 / (1.0 + jnp.exp(-pre))
    slope[...] = logistic * (1.0 + pre * (1.0 - logistic))
    hid[g] = (pre * logistic).astype(jnp.bfloat16)
    for d, peer in enumerate(dp_peers):
        push(hid.at[g], hid.at[g], h_send.at[d], h_recv.at[g], (peer, e))
    cols_t[g] = recv_t[:, :, own]

    for i, source in enumerate(sources):
        arrived(recv_s.at[source], s_send.at[i], s_recv.at[source])
        forward(recv_s, cols_s, source, cs_send, cs_recv, i)
    down_copy.wait()
    hidden_grad = jnp.dot(recv_s[...].reshape(total, width), down[...],
                          preferred_element_type=jnp.float32)
    pgr[g] = (hidden_grad * slope[...]).astype(jnp.bfloat16)
    for d, peer in enumerate(dp_peers):
        push(pgr.at[g], pgr.at[g], p_send.at[d], p_recv.at[g], (peer, e))

    chunk = width // RETURN_CHUNKS
    for c in range(RETURN_CHUNKS):
        piece = lax.dot_general(
            pgr[g], up[pl.ds(c * chunk, chunk), :], (((1,), (1,)), ((), ())),
            preferred_element_type=jnp.float32).astype(jnp.bfloat16)
        stage_o[c] = piece.reshape(blocks, rows, chunk)
        for i, peer in enumerate(peers):
            push(stage_o.at[c, peer], ret.at[c, e],
                 r_send.at[c, i], r_recv.at[c, e], (g, peer))
        ret[c, e] = stage_o[c, e]

    raw = jnp.sum(hid[g].astype(jnp.float32) * hidden_grad, axis=1, keepdims=True)
    spread = jnp.where(row_id % rows == lane_id % rows, raw, 0.0)
    gate_stage[...] = jnp.sum(
        spread.reshape(blocks, rows, total), axis=1, keepdims=True)
    for i, peer in enumerate(peers):
        push(gate_stage.at[peer], gret.at[e], g_send.at[i], g_recv.at[e], (g, peer))
    gret[e] = gate_stage[e]
    cols_s[g] = recv_s[:, :, own]

    contract_rows = (((0,), (0,)), ((), ()))
    for source in dp_sources:
        for block in range(n_ex):
            arrived(cols_s.at[source, block], cs_send.at[0, 0], cs_recv.at[source, block])
        arrived(hid.at[source], h_send.at[0], h_recv.at[source])
    gd_ref[0] = lax.dot_general(
        cols_s[...].reshape(n_dp * total, share),
        hid[...].reshape(n_dp * total, hidden_width), contract_rows,
        preferred_element_type=jnp.float32).astype(jnp.bfloat16)
    for source in dp_sources:
        for block in range(n_ex):
            arrived(cols_t.at[source, block], ct_send.at[0, 0], ct_recv.at[source, block])
        arrived(pgr.at[source], p_send.at[0], p_recv.at[source])
    gu_ref[0] = lax.dot_general(
        cols_t[...].reshape(n_dp * total, share),
        pgr[...].reshape(n_dp * total, hidden_width), contract_rows,
        preferred_element_type=jnp.float32).astype(jnp.bfloat16)

    for i, source in enumerate(sources):
        arrived(gret.at[source], g_send.at[i], g_recv.at[source])
        for c in range(RETURN_CHUNKS):
            arrived(ret.at[c, source], r_send.at[c, i], r_recv.at[c, source])
    lanes = lax.broadcasted_iota(jnp.int32, (1, total), 1) // rows
    gate_sum = jnp.zeros((1, total), jnp.float32)
    for b in range(blocks):
        for c in range(RETURN_CHUNKS):
            tg_ref[b, :, c * chunk:(c + 1) * chunk] = ret[c, slots[b]]
        gate_sum = jnp.where(lanes == b, gret[slots[b]], gate_sum)
    gg_ref[...] = (gate_sum / gate_row).astype(jnp.bfloat16)
    for copy in sends:
        copy.wait_send()


def fused(tokens, cotangent, gate_score, block_expert, expert_slot, up_weight, down_weight):
    n_dp = lax.axis_size("dp")
    n_ex = lax.axis_size("expert")
    total, width = tokens.shape
    hidden_width = up_weight.shape[2]
    blocks = block_expert.shape[0]
    rows = total // blocks
    share = width // n_dp
    chunk = width // RETURN_CHUNKS
    bf16 = jnp.bfloat16
    dma = pltpu.SemaphoreType.DMA
    vmem = pl.BlockSpec(memory_space=pltpu.VMEM)
    smem = pl.BlockSpec(memory_space=pltpu.SMEM)
    hbm = pl.BlockSpec(memory_space=pl.ANY)
    grouped = (blocks, rows, width)
    token_grad, gate_grad, grad_up, grad_down = pl.pallas_call(
        functools.partial(fused_kernel, n_dp, n_ex),
        out_shape=(
            jax.ShapeDtypeStruct(grouped, bf16),
            jax.ShapeDtypeStruct((1, total), bf16),
            jax.ShapeDtypeStruct((1, share, hidden_width), bf16),
            jax.ShapeDtypeStruct((1, share, hidden_width), bf16),
        ),
        in_specs=[smem, smem, vmem, vmem, vmem, hbm, hbm],
        out_specs=(vmem, vmem, vmem, vmem),
        scratch_shapes=[
            pltpu.VMEM((width, hidden_width), bf16),
            pltpu.VMEM((width, hidden_width), bf16),
            pltpu.VMEM((blocks, rows, 128), jnp.float32),
            pltpu.VMEM((n_ex - 1, rows, width), bf16),
            pltpu.VMEM((n_ex - 1, rows, width), bf16),
            pltpu.VMEM((n_ex, rows, width), bf16),
            pltpu.VMEM((n_ex, rows, width), bf16),
            pltpu.VMEM((n_dp, n_ex, rows, share), bf16),
            pltpu.VMEM((n_dp, n_ex, rows, share), bf16),
            pltpu.VMEM((n_dp, total, hidden_width), bf16),
            pltpu.VMEM((n_dp, total, hidden_width), bf16),
            pltpu.VMEM((total, hidden_width), jnp.float32),
            pltpu.VMEM((RETURN_CHUNKS, n_ex, rows, chunk), bf16),
            pltpu.VMEM((RETURN_CHUNKS, n_ex, rows, chunk), bf16),
            pltpu.VMEM((n_ex, 1, total), jnp.float32),
            pltpu.VMEM((n_ex, 1, total), jnp.float32),
            dma((2,)),
            dma((n_ex,)), dma((n_ex,)), dma((n_ex,)), dma((n_ex,)),
            dma((n_dp, n_ex)), dma((n_dp, n_ex)), dma((n_dp, n_ex)), dma((n_dp, n_ex)),
            dma((n_dp,)), dma((n_dp,)), dma((n_dp,)), dma((n_dp,)),
            dma((RETURN_CHUNKS, n_ex)), dma((RETURN_CHUNKS, n_ex)),
            dma((n_ex,)), dma((n_ex,)),
        ],
        compiler_params=pltpu.CompilerParams(
            collective_id=0, has_side_effects=True, vmem_limit_bytes=48 << 20),
        name="fused_layer",
    )(block_expert, expert_slot, gate_score.reshape(1, total),
      tokens.reshape(grouped), cotangent.reshape(grouped), up_weight, down_weight)
    return token_grad.reshape(total, width), gate_grad.reshape(total), grad_up, grad_down


def silu_slope(pre_act):
    logistic = jax.nn.sigmoid(pre_act)
    return logistic * (1.0 + pre_act * (1.0 - logistic))


def arrange(values, order_index, peer_count):
    shaped = values.reshape((peer_count, values.shape[0] // peer_count) + values.shape[1:])
    return jnp.take(shaped, order_index, axis=0).reshape(values.shape)


def local(tokens, cotangent, gate_score, block_expert, expert_slot, up_weight, down_weight):
    row_count, model_width = tokens.shape
    hidden_width = up_weight.shape[2]
    peer_count = lax.axis_size("expert")
    share_rows = model_width // lax.axis_size("dp")
    expert_count = expert_slot.shape[0]
    chosen = (block_expert[:, None] == jnp.arange(expert_count, dtype=jnp.int32)[None, :]).astype(
        jnp.int32
    )
    block_slot = jnp.sum(chosen * expert_slot[None, :], axis=1)
    places = jnp.arange(peer_count, dtype=jnp.int32)
    matches = (block_slot[None, :] == places[:, None]).astype(jnp.int32)
    source = jnp.sum(matches * places[None, :], axis=1)
    outbound = (
        arrange(tokens, source, peer_count),
        arrange(cotangent, source, peer_count),
        arrange(gate_score, source, peer_count),
    )
    inputs, upstream, gate_rows = (
        lax.all_to_all(outbound[0], "expert", split_axis=0, concat_axis=0, tiled=True),
        lax.all_to_all(outbound[1], "expert", split_axis=0, concat_axis=0, tiled=True),
        lax.all_to_all(outbound[2], "expert", split_axis=0, concat_axis=0, tiled=True),
    )
    up_mat = up_weight[0]
    down_mat = down_weight[0]
    contract_last = (((1,), (1,)), ((), ()))
    pre_act = jnp.dot(inputs, up_mat, preferred_element_type=jnp.float32)
    hidden = jax.nn.silu(pre_act).astype(jnp.bfloat16)
    expert_out = lax.dot_general(
        hidden, down_mat, contract_last, preferred_element_type=jnp.float32
    )
    gate_grad = jnp.sum(upstream.astype(jnp.float32) * expert_out, axis=1).astype(jnp.bfloat16)
    scaled = (gate_rows.astype(jnp.float32)[:, None] * upstream.astype(jnp.float32)).astype(
        jnp.bfloat16
    )
    hidden_grad = jnp.dot(scaled, down_mat, preferred_element_type=jnp.float32)
    pre_grad = (hidden_grad * silu_slope(pre_act)).astype(jnp.bfloat16)
    input_grad = lax.dot_general(
        pre_grad, up_mat, contract_last, preferred_element_type=jnp.float32
    ).astype(jnp.bfloat16)
    returned, gate_back = (
        lax.all_to_all(input_grad, "expert", split_axis=0, concat_axis=0, tiled=True),
        lax.all_to_all(gate_grad, "expert", split_axis=0, concat_axis=0, tiled=True),
    )
    columns = (
        lax.all_to_all(inputs, "dp", split_axis=1, concat_axis=0, tiled=True),
        lax.all_to_all(scaled, "dp", split_axis=1, concat_axis=0, tiled=True),
    )
    pieces = (
        lax.all_gather(pre_grad, "dp", axis=0, tiled=True),
        lax.all_gather(hidden, "dp", axis=0, tiled=True),
    )
    row_total = pieces[0].shape[0]
    shards = row_total // row_count
    input_rows = columns[0].reshape(shards, row_count, share_rows)
    scaled_rows = columns[1].reshape(shards, row_count, share_rows)
    grad_rows = pieces[0].reshape(shards, row_count, hidden_width)
    hidden_rows = pieces[1].reshape(shards, row_count, hidden_width)
    up_partial = jnp.einsum(
        "krc,krh->kch", input_rows, grad_rows, preferred_element_type=jnp.float32
    ).astype(jnp.bfloat16)
    down_partial = jnp.einsum(
        "krc,krh->kch", scaled_rows, hidden_rows, preferred_element_type=jnp.float32
    ).astype(jnp.bfloat16)
    grad_up = jnp.sum(up_partial.astype(jnp.float32), axis=0)
    grad_down = jnp.sum(down_partial.astype(jnp.float32), axis=0)
    token_grad = arrange(returned, block_slot, peer_count)
    gate_out = arrange(gate_back, block_slot, peer_count)
    return (
        token_grad,
        gate_out,
        grad_up.astype(jnp.bfloat16)[None],
        grad_down.astype(jnp.bfloat16)[None],
    )


def solution(mesh):
    def layer(*args):
        blocks = args[3].shape[0]
        rows = args[0].shape[0] // blocks
        share = args[0].shape[1] // mesh.shape["dp"]
        tiled = rows % 16 == 0 and share % 128 == 0 and args[0].shape[0] == 128
        same = blocks == mesh.shape["expert"] == args[4].shape[0]
        return fused(*args) if tiled and same else local(*args)

    return jax.shard_map(
        layer,
        mesh=mesh,
        in_specs=(
            P(("dp", "expert"), None),
            P(("dp", "expert"), None),
            P(("dp", "expert")),
            P(("dp", "expert")),
            P(),
            P("expert", None, None),
            P("expert", None, None),
        ),
        out_specs=(
            P(("dp", "expert"), None),
            P(("dp", "expert")),
            P("expert", "dp", None),
            P("expert", "dp", None),
        ),
        check_vma=False,
    )
```

```python
import functools

import jax
import jax.numpy as jnp
from jax import lax
from jax.experimental import pallas as pl
from jax.experimental.pallas import tpu as pltpu
from jax.sharding import PartitionSpec as P

MESH = pl.DeviceIdType.MESH
RETURN_CHUNKS = 2


def fused_kernel(
    n_dp, n_ex,
    block_expert, expert_slot, gate_ref, tok_ref, cot_ref, up_hbm, down_hbm,
    tg_ref, gg_ref, gu_ref, gd_ref,
    up, down, gcol, stage_t, stage_s, recv_t, recv_s, cols_t, cols_s,
    hid, pgr, slope, stage_o, ret, gate_stage, gret,
    w_sem, t_send, t_recv, s_send, s_recv, ct_send, ct_recv, cs_send, cs_recv,
    h_send, h_recv, p_send, p_recv, r_send, r_recv, g_send, g_recv,
):
    blocks, rows, width = tok_ref.shape
    total = blocks * rows
    hidden_width = up.shape[0]
    share = width // n_dp
    g = lax.axis_index("dp")
    e = lax.axis_index("expert")
    up_copy = pltpu.make_async_copy(up_hbm.at[0], up, w_sem.at[0])
    down_copy = pltpu.make_async_copy(down_hbm.at[0], down, w_sem.at[1])
    up_copy.start()
    down_copy.start()

    steps = sorted(range(1, n_ex), key=lambda k: abs(2 * k - n_ex))
    peers = [lax.rem(e + k, n_ex) for k in steps]
    sources = [lax.rem(e + n_ex - k, n_ex) for k in steps]
    dp_steps = sorted(range(1, n_dp), key=lambda k: abs(2 * k - n_dp))
    dp_peers = [lax.rem(g + k, n_dp) for k in dp_steps]
    dp_sources = [lax.rem(g + n_dp - k, n_dp) for k in dp_steps]

    barrier = pltpu.get_barrier_semaphore()
    for peer in peers:
        pl.semaphore_signal(barrier, inc=1, device_id=(g, peer), device_id_type=MESH)
    for peer in dp_peers:
        pl.semaphore_signal(barrier, inc=1, device_id=(peer, e), device_id_type=MESH)

    slots = [expert_slot[block_expert[b]] for b in range(blocks)]

    def source_block(slot):
        found = jnp.int32(0)
        for b in range(blocks):
            found = jnp.where(slots[b] == slot, jnp.int32(b), found)
        return found

    own_block = source_block(e)
    picks = [source_block(peer) for peer in peers]

    gate_row = gate_ref[...].astype(jnp.float32)
    row_id = lax.broadcasted_iota(jnp.int32, (total, total), 0)
    lane_id = lax.broadcasted_iota(jnp.int32, (total, total), 1)
    column = jnp.sum(jnp.where(row_id == lane_id, gate_row, 0.0), axis=1, keepdims=True)
    gcol[...] = jnp.broadcast_to(column, (total, 128)).reshape(blocks, rows, 128)

    for i, pick in enumerate(picks):
        stage_t[i] = tok_ref[pick]
    pl.semaphore_wait(barrier, n_ex - 1 + n_dp - 1)

    sends = []

    def push(src, dst, send_sem, recv_sem, device):
        copy = pltpu.make_async_remote_copy(
            src_ref=src, dst_ref=dst, send_sem=send_sem, recv_sem=recv_sem,
            device_id=device, device_id_type=MESH)
        copy.start()
        sends.append(copy)

    def arrived(ref, send_sem, recv_sem):
        pltpu.make_async_remote_copy(
            src_ref=ref, dst_ref=ref, send_sem=send_sem, recv_sem=recv_sem,
            device_id=(g, peers[0]), device_id_type=MESH).wait_recv()

    for i, peer in enumerate(peers):
        push(stage_t.at[i], recv_t.at[e], t_send.at[i], t_recv.at[e], (g, peer))

    def scale(pick):
        factor = gcol[pick][:, :1]
        return (cot_ref[pick].astype(jnp.float32) * factor).astype(jnp.bfloat16)

    for i, peer in enumerate(peers):
        stage_s[i] = scale(picks[i])
        push(stage_s.at[i], recv_s.at[e], s_send.at[i], s_recv.at[e], (g, peer))
    recv_t[e] = tok_ref[own_block]
    recv_s[e] = scale(own_block)

    def forward(recv, cols, block, send_sem, recv_sem, i):
        for d, peer in enumerate(dp_peers):
            window = pl.ds(pl.multiple_of(peer * share, share), share)
            push(recv.at[block, :, window], cols.at[g, block],
                 send_sem.at[d, i], recv_sem.at[g, block], (peer, e))

    own = pl.ds(pl.multiple_of(g * share, share), share)

    forward(recv_t, cols_t, e, ct_send, ct_recv, n_ex - 1)
    forward(recv_s, cols_s, e, cs_send, cs_recv, n_ex - 1)
    for i, source in enumerate(sources):
        arrived(recv_t.at[source], t_send.at[i], t_recv.at[source])
        forward(recv_t, cols_t, source, ct_send, ct_recv, i)
    up_copy.wait()
    contract_last = (((1,), (1,)), ((), ()))
    pre = lax.dot_general(recv_t[...].reshape(total, width), up[...], contract_last,
                          preferred_element_type=jnp.float32)
    logistic = 1.0 / (1.0 + jnp.exp(-pre))
    slope[...] = logistic * (1.0 + pre * (1.0 - logistic))
    hid[g] = (pre * logistic).astype(jnp.bfloat16)
    for d, peer in enumerate(dp_peers):
        push(hid.at[g], hid.at[g], h_send.at[d], h_recv.at[g], (peer, e))
    cols_t[g] = recv_t[:, :, own]

    for i, source in enumerate(sources):
        arrived(recv_s.at[source], s_send.at[i], s_recv.at[source])
        forward(recv_s, cols_s, source, cs_send, cs_recv, i)
    down_copy.wait()
    hidden_grad = lax.dot_general(recv_s[...].reshape(total, width), down[...],
                                  contract_last, preferred_element_type=jnp.float32)
    pgr[g] = (hidden_grad * slope[...]).astype(jnp.bfloat16)
    for d, peer in enumerate(dp_peers):
        push(pgr.at[g], pgr.at[g], p_send.at[d], p_recv.at[g], (peer, e))

    chunk = width // RETURN_CHUNKS
    for c in range(RETURN_CHUNKS):
        piece = jnp.dot(pgr[g], up[:, c * chunk:(c + 1) * chunk],
                        preferred_element_type=jnp.float32).astype(jnp.bfloat16)
        stage_o[c] = piece.reshape(blocks, rows, chunk)
        for i, peer in enumerate(peers):
            push(stage_o.at[c, peer], ret.at[c, e],
                 r_send.at[c, i], r_recv.at[c, e], (g, peer))
        ret[c, e] = stage_o[c, e]

    raw = jnp.sum(hid[g].astype(jnp.float32) * hidden_grad, axis=1, keepdims=True)
    spread = jnp.where(row_id % rows == lane_id % rows, raw, 0.0)
    gate_stage[...] = jnp.sum(
        spread.reshape(blocks, rows, total), axis=1, keepdims=True)
    for i, peer in enumerate(peers):
        push(gate_stage.at[peer], gret.at[e], g_send.at[i], g_recv.at[e], (g, peer))
    gret[e] = gate_stage[e]
    cols_s[g] = recv_s[:, :, own]

    contract_rows = (((0,), (0,)), ((), ()))
    for source in dp_sources:
        for block in range(n_ex):
            arrived(cols_s.at[source, block], cs_send.at[0, 0], cs_recv.at[source, block])
        arrived(hid.at[source], h_send.at[0], h_recv.at[source])
    gd_ref[0] = lax.dot_general(
        hid[...].reshape(n_dp * total, hidden_width),
        cols_s[...].reshape(n_dp * total, share), contract_rows,
        preferred_element_type=jnp.float32).astype(jnp.bfloat16)
    for source in dp_sources:
        for block in range(n_ex):
            arrived(cols_t.at[source, block], ct_send.at[0, 0], ct_recv.at[source, block])
        arrived(pgr.at[source], p_send.at[0], p_recv.at[source])
    gu_ref[0] = lax.dot_general(
        pgr[...].reshape(n_dp * total, hidden_width),
        cols_t[...].reshape(n_dp * total, share), contract_rows,
        preferred_element_type=jnp.float32).astype(jnp.bfloat16)

    for i, source in enumerate(sources):
        arrived(gret.at[source], g_send.at[i], g_recv.at[source])
        for c in range(RETURN_CHUNKS):
            arrived(ret.at[c, source], r_send.at[c, i], r_recv.at[c, source])
    lanes = lax.broadcasted_iota(jnp.int32, (1, total), 1) // rows
    gate_sum = jnp.zeros((1, total), jnp.float32)
    for b in range(blocks):
        for c in range(RETURN_CHUNKS):
            tg_ref[b, :, c * chunk:(c + 1) * chunk] = ret[c, slots[b]]
        gate_sum = jnp.where(lanes == b, gret[slots[b]], gate_sum)
    gg_ref[...] = (gate_sum / gate_row).astype(jnp.bfloat16)
    for copy in sends:
        copy.wait_send()


def fused(tokens, cotangent, gate_score, block_expert, expert_slot, up_weight, down_weight):
    n_dp = lax.axis_size("dp")
    n_ex = lax.axis_size("expert")
    total, width = tokens.shape
    hidden_width = up_weight.shape[2]
    blocks = block_expert.shape[0]
    rows = total // blocks
    share = width // n_dp
    chunk = width // RETURN_CHUNKS
    bf16 = jnp.bfloat16
    dma = pltpu.SemaphoreType.DMA
    vmem = pl.BlockSpec(memory_space=pltpu.VMEM)
    smem = pl.BlockSpec(memory_space=pltpu.SMEM)
    hbm = pl.BlockSpec(memory_space=pl.ANY)
    grouped = (blocks, rows, width)
    token_grad, gate_grad, grad_up, grad_down = pl.pallas_call(
        functools.partial(fused_kernel, n_dp, n_ex),
        out_shape=(
            jax.ShapeDtypeStruct(grouped, bf16),
            jax.ShapeDtypeStruct((1, total), bf16),
            jax.ShapeDtypeStruct((1, hidden_width, share), bf16),
            jax.ShapeDtypeStruct((1, hidden_width, share), bf16),
        ),
        in_specs=[smem, smem, vmem, vmem, vmem, hbm, hbm],
        out_specs=(vmem, vmem, vmem, vmem),
        scratch_shapes=[
            pltpu.VMEM((hidden_width, width), bf16),
            pltpu.VMEM((hidden_width, width), bf16),
            pltpu.VMEM((blocks, rows, 128), jnp.float32),
            pltpu.VMEM((n_ex - 1, rows, width), bf16),
            pltpu.VMEM((n_ex - 1, rows, width), bf16),
            pltpu.VMEM((n_ex, rows, width), bf16),
            pltpu.VMEM((n_ex, rows, width), bf16),
            pltpu.VMEM((n_dp, n_ex, rows, share), bf16),
            pltpu.VMEM((n_dp, n_ex, rows, share), bf16),
            pltpu.VMEM((n_dp, total, hidden_width), bf16),
            pltpu.VMEM((n_dp, total, hidden_width), bf16),
            pltpu.VMEM((total, hidden_width), jnp.float32),
            pltpu.VMEM((RETURN_CHUNKS, n_ex, rows, chunk), bf16),
            pltpu.VMEM((RETURN_CHUNKS, n_ex, rows, chunk), bf16),
            pltpu.VMEM((n_ex, 1, total), jnp.float32),
            pltpu.VMEM((n_ex, 1, total), jnp.float32),
            dma((2,)),
            dma((n_ex,)), dma((n_ex,)), dma((n_ex,)), dma((n_ex,)),
            dma((n_dp, n_ex)), dma((n_dp, n_ex)), dma((n_dp, n_ex)), dma((n_dp, n_ex)),
            dma((n_dp,)), dma((n_dp,)), dma((n_dp,)), dma((n_dp,)),
            dma((RETURN_CHUNKS, n_ex)), dma((RETURN_CHUNKS, n_ex)),
            dma((n_ex,)), dma((n_ex,)),
        ],
        compiler_params=pltpu.CompilerParams(
            collective_id=0, has_side_effects=True, vmem_limit_bytes=48 << 20),
        name="fused_layer",
    )(block_expert, expert_slot, gate_score.reshape(1, total),
      tokens.reshape(grouped), cotangent.reshape(grouped),
      jnp.swapaxes(up_weight, 1, 2), jnp.swapaxes(down_weight, 1, 2))
    return (token_grad.reshape(total, width), gate_grad.reshape(total),
            jnp.swapaxes(grad_up, 1, 2), jnp.swapaxes(grad_down, 1, 2))


def silu_slope(pre_act):
    logistic = jax.nn.sigmoid(pre_act)
    return logistic * (1.0 + pre_act * (1.0 - logistic))


def arrange(values, order_index, peer_count):
    shaped = values.reshape((peer_count, values.shape[0] // peer_count) + values.shape[1:])
    return jnp.take(shaped, order_index, axis=0).reshape(values.shape)


def local(tokens, cotangent, gate_score, block_expert, expert_slot, up_weight, down_weight):
    row_count, model_width = tokens.shape
    hidden_width = up_weight.shape[2]
    peer_count = lax.axis_size("expert")
    share_rows = model_width // lax.axis_size("dp")
    expert_count = expert_slot.shape[0]
    chosen = (block_expert[:, None] == jnp.arange(expert_count, dtype=jnp.int32)[None, :]).astype(
        jnp.int32
    )
    block_slot = jnp.sum(chosen * expert_slot[None, :], axis=1)
    places = jnp.arange(peer_count, dtype=jnp.int32)
    matches = (block_slot[None, :] == places[:, None]).astype(jnp.int32)
    source = jnp.sum(matches * places[None, :], axis=1)
    outbound = (
        arrange(tokens, source, peer_count),
        arrange(cotangent, source, peer_count),
        arrange(gate_score, source, peer_count),
    )
    inputs, upstream, gate_rows = (
        lax.all_to_all(outbound[0], "expert", split_axis=0, concat_axis=0, tiled=True),
        lax.all_to_all(outbound[1], "expert", split_axis=0, concat_axis=0, tiled=True),
        lax.all_to_all(outbound[2], "expert", split_axis=0, concat_axis=0, tiled=True),
    )
    up_mat = up_weight[0]
    down_mat = down_weight[0]
    contract_last = (((1,), (1,)), ((), ()))
    pre_act = jnp.dot(inputs, up_mat, preferred_element_type=jnp.float32)
    hidden = jax.nn.silu(pre_act).astype(jnp.bfloat16)
    expert_out = lax.dot_general(
        hidden, down_mat, contract_last, preferred_element_type=jnp.float32
    )
    gate_grad = jnp.sum(upstream.astype(jnp.float32) * expert_out, axis=1).astype(jnp.bfloat16)
    scaled = (gate_rows.astype(jnp.float32)[:, None] * upstream.astype(jnp.float32)).astype(
        jnp.bfloat16
    )
    hidden_grad = jnp.dot(scaled, down_mat, preferred_element_type=jnp.float32)
    pre_grad = (hidden_grad * silu_slope(pre_act)).astype(jnp.bfloat16)
    input_grad = lax.dot_general(
        pre_grad, up_mat, contract_last, preferred_element_type=jnp.float32
    ).astype(jnp.bfloat16)
    returned, gate_back = (
        lax.all_to_all(input_grad, "expert", split_axis=0, concat_axis=0, tiled=True),
        lax.all_to_all(gate_grad, "expert", split_axis=0, concat_axis=0, tiled=True),
    )
    columns = (
        lax.all_to_all(inputs, "dp", split_axis=1, concat_axis=0, tiled=True),
        lax.all_to_all(scaled, "dp", split_axis=1, concat_axis=0, tiled=True),
    )
    pieces = (
        lax.all_gather(pre_grad, "dp", axis=0, tiled=True),
        lax.all_gather(hidden, "dp", axis=0, tiled=True),
    )
    row_total = pieces[0].shape[0]
    shards = row_total // row_count
    input_rows = columns[0].reshape(shards, row_count, share_rows)
    scaled_rows = columns[1].reshape(shards, row_count, share_rows)
    grad_rows = pieces[0].reshape(shards, row_count, hidden_width)
    hidden_rows = pieces[1].reshape(shards, row_count, hidden_width)
    up_partial = jnp.einsum(
        "krc,krh->kch", input_rows, grad_rows, preferred_element_type=jnp.float32
    ).astype(jnp.bfloat16)
    down_partial = jnp.einsum(
        "krc,krh->kch", scaled_rows, hidden_rows, preferred_element_type=jnp.float32
    ).astype(jnp.bfloat16)
    grad_up = jnp.sum(up_partial.astype(jnp.float32), axis=0)
    grad_down = jnp.sum(down_partial.astype(jnp.float32), axis=0)
    token_grad = arrange(returned, block_slot, peer_count)
    gate_out = arrange(gate_back, block_slot, peer_count)
    return (
        token_grad,
        gate_out,
        grad_up.astype(jnp.bfloat16)[None],
        grad_down.astype(jnp.bfloat16)[None],
    )


def solution(mesh):
    def layer(*args):
        blocks = args[3].shape[0]
        rows = args[0].shape[0] // blocks
        share = args[0].shape[1] // mesh.shape["dp"]
        tiled = rows % 16 == 0 and share % 128 == 0 and args[0].shape[0] == 128
        same = blocks == mesh.shape["expert"] == args[4].shape[0]
        return fused(*args) if tiled and same else local(*args)

    return jax.shard_map(
        layer,
        mesh=mesh,
        in_specs=(
            P(("dp", "expert"), None),
            P(("dp", "expert"), None),
            P(("dp", "expert")),
            P(("dp", "expert")),
            P(),
            P("expert", None, None),
            P("expert", None, None),
        ),
        out_specs=(
            P(("dp", "expert"), None),
            P(("dp", "expert")),
            P("expert", "dp", None),
            P("expert", "dp", None),
        ),
        check_vma=False,
    )
```
